128 devices in a mesh: row: 8 (over x, y_lo), col: 16 (over z, y_hi, core).
Axes of the slice: x: 4, y: 4 (y_hi: 2, y_lo: 2; y = y_hi * 2 + y_lo), z: 4, core: 2. Of those that a mesh axis runs over, the one named last changes fastest.
Arguments:
- atom_blocks: float32 [128, 16, 128, 128], P('row', 'col'), may hold values from -6 to 6
- grid_position: int32 [128], replicated, may hold values from 0 to 127, as said below
- pattern: int32 [128, 16], replicated, may hold values from -1 to 127, as said below
Outputs:
- square: float32 [128, 16, 128, 128], P('row', 'col')
- update: float32 [128, 16, 128, 128], P('row', 'col')
The draws below stay inside these ranges and needn't reach their ends.
Inputs may be any that keep to these rules, and one draw needn't show every extreme that they name: grid_position is a permutation; the 16 atom block rows a with a // 16 equal put at most 2 grid positions into any one run of 16 grid positions that starts at a multiple of 16, and exactly 2 into some run. `pattern`: each row holds 12 different block columns, one of them its own index, and -1 in its other slots; all slots s that hold one block column j have the same s; the block rows lie on a cycle of 128 places, not given, on which each row's columns lie within 16 places in a row around its own.
All inputs are finite; a program needn't handle non-finite values.
Results may differ from the reference program's by a relative error of at most 0.0003.
Values sent between devices are 32-bit elements; how exact they have to be, the bound alone decides.
No kernel may reach another device: no remote copies, remote signals or barrier semaphores. Data moves between devices by JAX's collectives and lax.ppermute only.
A program may use at most 128 MiB of HBM per device.

```python
import math
import jax
import jax.numpy as jnp
from jax import lax

BLOCK = 128
NZ = 12
NBG = 16
NB = 128
SLOT = 1
NS = 16


def slot_order(subkey):
    return jax.random.permutation(subkey, NBG)


def offset_order(subkey):
    return jax.random.permutation(subkey, NS - 1)


def make_layout(key):
    base_key = jax.random.fold_in(key, 17)
    key_groups, key_slots, key_cycle, key_picks = jax.random.split(base_key, 4)
    groups = NB // NBG
    shuffle = jax.random.permutation(key_groups, groups).astype(jnp.int32)
    slot_values = jax.vmap(slot_order)(jax.random.split(key_slots, groups)).astype(jnp.int32)
    source = jnp.arange(groups, dtype=jnp.int32)[:, None]
    target = shuffle[(source + slot_values // 2) % groups]
    sort_key = (target * NB + source * NBG + slot_values).reshape(-1)
    ordering = jnp.argsort(sort_key)
    position = jnp.argsort(ordering).astype(jnp.int32)
    cycle_place = jax.random.permutation(key_cycle, NB).astype(jnp.int32)
    cycle_atoms = jnp.argsort(cycle_place).astype(jnp.int32)
    offsets = jnp.arange(NS, dtype=jnp.int32)
    places = (cycle_place[:, None] - NS // 2 + 1 + offsets[None, :]) % NB
    columns = cycle_atoms[places]
    ranking = jax.vmap(offset_order)(jax.random.split(key_picks, NB)).astype(jnp.int32)
    lookup = jnp.where(offsets < NS // 2 - 1, offsets, offsets - 1)
    lookup = jnp.clip(lookup, 0, NS - 2)
    chosen = (jnp.take(ranking, lookup, axis=1) < NZ - 1) | (offsets == NS // 2 - 1)[None, :]
    col_groups = NS // SLOT
    slot_index = places % col_groups * SLOT + offsets[None, :] // col_groups
    values = jnp.where(chosen, columns, -1).astype(jnp.int32)
    row_numbers = jnp.arange(NB, dtype=jnp.int32)[:, None]
    pattern = jnp.full((NB, NS), -1, jnp.int32).at[row_numbers, slot_index].set(values)
    return (position, pattern)


def draw_grid_position(key, part):
    return make_layout(key)[0]


def draw_pattern(key, part):
    return make_layout(key)[1]


def block_scale(rng, extent, pieces, smallest, high):
    def one(axis_at, blocks):
        heights = jax.random.uniform(jax.random.fold_in(jax.random.fold_in(rng, 6), axis_at), (blocks,), jnp.float32, smallest / len(pieces), high / len(pieces))
        return jnp.repeat(jnp.exp(heights), extent[axis_at] // blocks).reshape((-1,) + (1,) * (len(extent) - axis_at - 1))

    level = one(*pieces[0])
    for cut in pieces[1:]:
        level = level * one(*cut)
    return level


def bell_draw(rng, shape, width, bound, pieces=(), held_as=jnp.bfloat16):
    drawn = width * jax.random.normal(rng, shape, jnp.float32)
    if pieces:
        drawn = drawn * block_scale(rng, shape, pieces, -0.22, 0.18)
    return jnp.clip(drawn, -bound, bound).astype(held_as)


def setup_inputs(seed: int = 0) -> dict:
    arg_keys = jax.random.split(jax.random.key(seed), 4)
    return {
        "atom_blocks": bell_draw(arg_keys[0], (NB, NS, BLOCK, BLOCK), 1.0, 6.0, ((0, 8), (1, 16)), jnp.float32),
        "grid_position": draw_grid_position(jax.random.fold_in(arg_keys[3], 71), 0),
        "pattern": draw_pattern(jax.random.fold_in(arg_keys[3], 71), 0),
    }


HIGHEST = lax.Precision.HIGHEST

def restrict(left, right, pattern):

    def row_product(inputs):
        row_blocks, row_columns = inputs
        row_filled = row_columns >= 0
        neighbours = jnp.maximum(row_columns, 0)
        right_rows = right[neighbours]
        right_columns = pattern[neighbours]
        matches = (right_columns[:, :, None] == row_columns[None, None, :]) & row_filled[None, None, :] & row_filled[:, None, None]
        weights = jnp.einsum('uvt,uvpq->utpq', matches.astype(right.dtype), right_rows, precision=HIGHEST)
        return jnp.einsum('upq,utqr->tpr', row_blocks, weights, precision=HIGHEST)
    return lax.map(row_product, (left, pattern))

def reference(atom_blocks, grid_position, pattern):
    start_scale = 1.0 / math.sqrt(NZ * BLOCK)
    scale_back = math.sqrt(NZ * BLOCK)
    filled = (pattern >= 0)[:, :, None, None]
    matrix = jnp.where(filled, atom_blocks * start_scale, 0.0)
    masked_square = restrict(matrix, matrix, pattern)
    cubic = restrict(matrix, masked_square, pattern)
    square_atoms = masked_square * scale_back
    update_atoms = (1.5 * matrix - 0.5 * cubic) * scale_back
    square = jnp.zeros_like(square_atoms).at[grid_position].set(square_atoms)
    update = jnp.zeros_like(update_atoms).at[grid_position].set(update_atoms)
    return (square, update)
```

```python
import math

import jax
import jax.numpy as jnp
from jax import lax
from jax.experimental import pallas as pl
from jax.experimental.pallas import tpu as pltpu
from jax.sharding import PartitionSpec as P

AXES = ("row", "col")
NX, NYL, NZ_, NYH, NCORE = 4, 2, 4, 2, 2
ROWS = 16
SLOTS = 16
ATOMS = 128
EDGE = 128
HALF = 8


def _places():
    for x in range(NX):
        for yl in range(NYL):
            for z in range(NZ_):
                for yh in range(NYH):
                    for core in range(NCORE):
                        yield x, yl, z, yh, core


def _linear(x, yl, z, yh, core):
    return (x * NYL + yl) * (NZ_ * NYH * NCORE) + (z * NYH + yh) * NCORE + core


def _moves(step):
    return [(_linear(*p), _linear(*step(*p))) for p in _places()]


def _way(core):
    return 1 if core == 0 else -1


def _y_step(x, yl, z, yh, core):
    y = (yh * NYL + yl + _way(core)) % (NYL * NYH)
    return x, y % NYL, z, y // NYL, core


MOVE_XA = _moves(lambda x, yl, z, yh, c: ((x + _way(c)) % NX, yl, z, yh, c))
MOVE_XB = _moves(lambda x, yl, z, yh, c: ((x - _way(c)) % NX, yl, z, yh, c))
MOVE_YP = _moves(lambda x, yl, z, yh, c: (x, 1 - yl, z, yh, c))
MOVE_ZA = _moves(lambda x, yl, z, yh, c: (x, yl, (z + _way(c)) % NZ_, yh, c))
MOVE_ZB = _moves(lambda x, yl, z, yh, c: (x, yl, (z - _way(c)) % NZ_, yh, c))
MOVE_YA = _moves(_y_step)
MOVE_C = _moves(lambda x, yl, z, yh, c: (x, yl, z, yh, 1 - c))


def move(value, moves):
    return lax.ppermute(value, AXES, moves)


def after(value, *others):
    return lax.optimization_barrier((value, *others))[0]


def _split(value):
    high = value.astype(jnp.bfloat16)
    low = (value - high.astype(jnp.float32)).astype(jnp.bfloat16)
    return high, low


def _pick_kernel(table, *refs):
    n = len(refs) - 2
    pieces, out, sems = refs[:n], refs[n], refs[n + 1]
    copies = []
    for q in range(n):
        for s in range(2):
            e = q * 2 + s
            copies.append(
                pltpu.make_async_copy(
                    pieces[q].at[table[e]], out.at[table[2 * n + e]], sems.at[e]
                )
            )
    for c in copies:
        c.start()
    for c in copies:
        c.wait()


def pick_rows(pieces, table):
    n = len(pieces)
    return pl.pallas_call(
        _pick_kernel,
        out_shape=jax.ShapeDtypeStruct((2 * n, EDGE, EDGE), jnp.float32),
        in_specs=[pl.BlockSpec(memory_space=pltpu.SMEM)]
        + [pl.BlockSpec(memory_space=pltpu.HBM)] * n,
        out_specs=pl.BlockSpec(memory_space=pltpu.VMEM),
        scratch_shapes=[pltpu.SemaphoreType.DMA((2 * n,))],
        compiler_params=pltpu.CompilerParams(vmem_limit_bytes=VMEM_LIMIT),
        name="pick_rows",
    )(table, *pieces)


def _start_left(table, left, lbuf, lsem, base, rows):
    def row(local, carry):
        t = base + local
        for p in range(SLOTS):
            rank = table[t, p]

            @pl.when(rank >= 0)
            def _():
                pltpu.make_async_copy(
                    left[p].at[local], lbuf.at[t, rank], lsem.at[t, p]
                ).start()

        return carry

    lax.fori_loop(0, rows, row, 0)


def _product(table, lbuf, rpan, t, start, count):
    ls, rs = [], []
    for n in range(start, start + count):
        ls.append(lbuf[t, table[t, 2 * SLOTS + n]])
        rs.append(rpan[table[t, SLOTS + n]])
    lh, ll = _split(jnp.concatenate(ls, axis=1))
    rh, rl = _split(jnp.concatenate(rs, axis=0))
    four = jnp.dot(
        jnp.concatenate([lh, ll], axis=0),
        jnp.concatenate([rh, rl], axis=1),
        preferred_element_type=jnp.float32,
    )
    return (four[:EDGE, :EDGE] + (four[:EDGE, EDGE:] + four[EDGE:, :EDGE])) + four[
        EDGE:, EDGE:
    ]


def _row_product(table, lbuf, rpan, acc, t):
    total = table[t, 3 * SLOTS]

    @pl.when(total > 0)
    def _():
        acc[...] = _product(table, lbuf, rpan, t, 0, 8)

    @pl.when(total == 0)
    def _():
        acc[...] = jnp.zeros((EDGE, EDGE), jnp.float32)

    @pl.when(total > 8)
    def _():
        acc[...] += _product(table, lbuf, rpan, t, 8, 4)


def _wait_row(table, left, lbuf, lsem, t, local):
    for p in range(SLOTS):
        rank = table[t, p]

        @pl.when(rank >= 0)
        def _():
            pltpu.make_async_copy(
                left[p].at[local], lbuf.at[t, rank], lsem.at[t, p]
            ).wait()


def _square_kernel(scale, n_rows, table, *refs):
    left = refs[:SLOTS]
    right = refs[SLOTS : SLOTS + 8]
    out, lbuf, rpan, acc, lsem, rsem = refs[SLOTS + 8 :]
    per = right[0].shape[0]
    loads = [
        pltpu.make_async_copy(right[q], rpan.at[pl.ds(q * per, per)], rsem.at[q])
        for q in range(8)
    ]
    for c in loads:
        c.start()
    _start_left(table, left, lbuf, lsem, 0, n_rows)
    rpan[ATOMS] = jnp.zeros((EDGE, EDGE), jnp.float32)
    for c in loads:
        c.wait()

    def row(t, carry):
        _wait_row(table, left, lbuf, lsem, t, t)
        _row_product(table, lbuf, rpan, acc, t)
        out[t] = acc[...] * scale
        return carry

    lax.fori_loop(0, n_rows, row, 0)


MOST = 12
VMEM_LIMIT = 58 * 2**20


def square_rows(table, left, right, scale):
    n_rows = left[0].shape[0]
    return pl.pallas_call(
        lambda *refs: _square_kernel(scale, n_rows, *refs),
        out_shape=jax.ShapeDtypeStruct((n_rows, EDGE, EDGE), jnp.float32),
        in_specs=[pl.BlockSpec(memory_space=pltpu.SMEM)]
        + [pl.BlockSpec(memory_space=pltpu.HBM)] * (SLOTS + 8),
        out_specs=pl.BlockSpec(memory_space=pltpu.VMEM),
        scratch_shapes=[
            pltpu.VMEM((n_rows, MOST, EDGE, EDGE), jnp.float32),
            pltpu.VMEM((ATOMS + 1, EDGE, EDGE), jnp.float32),
            pltpu.VMEM((EDGE, EDGE), jnp.float32),
            pltpu.SemaphoreType.DMA((n_rows, SLOTS)),
            pltpu.SemaphoreType.DMA((8,)),
        ],
        compiler_params=pltpu.CompilerParams(vmem_limit_bytes=VMEM_LIMIT),
        name="square_rows",
    )(table, *left, *right)


def _update_kernel(scale, table, *refs):
    left_a = refs[:SLOTS]
    left_b = refs[SLOTS : 2 * SLOTS]
    right = refs[2 * SLOTS : 2 * SLOTS + 16]
    square, update, lbuf, rpan, acc, ubuf, lsem, rsem, ssem, usem = refs[2 * SLOTS + 16 :]
    loads = [
        pltpu.make_async_copy(right[q], rpan.at[pl.ds(q * HALF, HALF)], rsem.at[q])
        for q in range(16)
    ]
    for c in loads:
        c.start()
    _start_left(table, left_a, lbuf, lsem, 0, HALF)
    _start_left(table, left_b, lbuf, lsem, HALF, HALF)
    rpan[ATOMS] = jnp.zeros((EDGE, EDGE), jnp.float32)
    for c in loads:
        c.wait()
    squares = [
        pltpu.make_async_copy(
            rpan.at[64 * (t // HALF) + t % HALF],
            square.at[table[t, 3 * SLOTS + 1]],
            ssem.at[t],
        )
        for t in range(ROWS)
    ]
    for c in squares:
        c.start()

    def put(t):
        return pltpu.make_async_copy(
            ubuf.at[t], update.at[table[t, 3 * SLOTS + 1]], usem.at[t]
        )

    def rows(left, base):
        def row(local, carry):
            t = base + local
            _wait_row(table, left, lbuf, lsem, t, local)
            _row_product(table, lbuf, rpan, acc, t)
            filled = table[t, 3 * SLOTS] > 0
            ubuf[t] = jnp.where(
                filled, 1.5 * lbuf[t, 0] - (0.5 * scale) * acc[...], 0.0
            )
            put(t).start()
            return carry

        lax.fori_loop(0, HALF, row, 0)

    rows(left_a, 0)
    rows(left_b, HALF)
    for t in range(ROWS):
        put(t).wait()
    for c in squares:
        c.wait()


def update_rows(table, left_a, left_b, right, scale):
    out = jax.ShapeDtypeStruct((ROWS, EDGE, EDGE), jnp.float32)
    hbm = pl.BlockSpec(memory_space=pltpu.HBM)
    return pl.pallas_call(
        lambda *refs: _update_kernel(scale, *refs),
        out_shape=(out, out),
        in_specs=[pl.BlockSpec(memory_space=pltpu.SMEM)] + [hbm] * (2 * SLOTS + 16),
        out_specs=(hbm, hbm),
        scratch_shapes=[
            pltpu.VMEM((ROWS, MOST, EDGE, EDGE), jnp.float32),
            pltpu.VMEM((ATOMS + 1, EDGE, EDGE), jnp.float32),
            pltpu.VMEM((EDGE, EDGE), jnp.float32),
            pltpu.VMEM((ROWS, EDGE, EDGE), jnp.float32),
            pltpu.SemaphoreType.DMA((ROWS, SLOTS)),
            pltpu.SemaphoreType.DMA((16,)),
            pltpu.SemaphoreType.DMA((ROWS,)),
            pltpu.SemaphoreType.DMA((ROWS,)),
        ],
        compiler_params=pltpu.CompilerParams(vmem_limit_bytes=VMEM_LIMIT),
        name="update_rows",
    )(table, *left_a, *left_b, *right)


def _mod4(v):
    return v & 3


def _order(dx, dy):
    return jnp.where(
        dy == 0,
        jnp.where(dx == 0, 0, jnp.where(dx == 1, 1, jnp.where(dx == 3, 2, 6))),
        jnp.where(dx == 0, 3, jnp.where(dx == 1, 4, jnp.where(dx == 3, 5, 7))),
    )


def _piece(dx, dy, way):
    return _order(_mod4(-way * dx), dy)


def _lookup(keys, values):
    atoms = jnp.arange(ATOMS, dtype=jnp.int32)
    return jnp.sum(jnp.where(keys[..., None] == atoms, values, 0), axis=-1)


def build_tables(grid_position, pattern):
    i32 = jnp.int32
    row = lax.axis_index("row").astype(i32)
    col = lax.axis_index("col").astype(i32)
    x, yl = row // 2, row % 2
    z, yh, core = col // 4, (col // 2) % 2, col % 2
    way = 1 - 2 * core
    atoms = jnp.arange(ATOMS, dtype=i32)
    eights = jnp.arange(8, dtype=i32)
    sixteen = jnp.arange(16, dtype=i32)
    group = atoms // ROWS
    target = grid_position // ROWS
    same = (group[:, None] == group[None, :]) & (target[:, None] == target[None, :])
    rank = jnp.sum((same & (atoms[None, :] < atoms[:, None])).astype(i32), axis=1)
    place = 2 * _order(
        _mod4(group // 2 - target // 2), (group % 2) ^ (target % 2)
    ) + rank
    mine = target == row
    local_atom = jnp.sum(
        jnp.where(mine[None, :] & (place[None, :] == sixteen[:, None]), atoms[None, :], 0),
        axis=1,
    )
    source = _piece(_mod4(group // 2 - x), (group % 2) ^ yl, way)
    pick = 2 * source + rank
    hit = mine[None, :] & (pick[None, :] == sixteen[:, None])
    pick_row = jnp.sum(jnp.where(hit, (atoms % ROWS)[None, :], 0), axis=1)
    pick_place = jnp.sum(jnp.where(hit, place[None, :], 0), axis=1)
    pick_first = jnp.concatenate([pick_row[:HALF], pick_place[:HALF]])
    pick_rest = jnp.concatenate([pick_row[HALF:], pick_place[HALF:] - HALF])
    right_first = source * ROWS + atoms % ROWS
    holder = _piece(_mod4(target // 2 - x), (target % 2) ^ yl, way)
    right_second = (place // HALF) * 64 + holder * HALF + place % HALF
    def slots(d, c):
        dz = jnp.stack([0 * d, -d, d, 0 * d, -d, d, 0 * d + 2, 0 * d + 2])
        flip = jnp.where(((eights >= 3) & (eights <= 5)) | (eights == 7), 1, 0)
        return _mod4(z + dz) * 4 + (yh ^ flip) * 2 + c

    slot_of = jnp.concatenate([slots(way, core), slots(-way, 1 - core)])
    column = lax.dynamic_slice_in_dim(pattern, col, 1, 1)[:, 0]
    local_pattern = jnp.sum(
        jnp.where((local_atom[:, None] == atoms)[:, :, None], pattern[None], 0), axis=1
    )
    ordered = jnp.sum(
        jnp.where((slot_of[:, None] == sixteen)[None], local_pattern[:, None, :], 0),
        axis=2,
    )
    mine_column = ordered[:, :1]
    match = (ordered >= 0) & (mine_column >= 0) & (_lookup(ordered, column) == mine_column)
    counts = match.astype(i32)
    before = jnp.sum(
        jnp.where(sixteen[None, None, :] < sixteen[None, :, None], counts[:, None, :], 0),
        axis=2,
    )
    total = jnp.sum(counts, axis=1)
    ranks = jnp.where(match, before, -1)
    chosen = ranks[:, None, :] == sixteen[None, :, None]
    used = sixteen[None, :] < total[:, None]
    left_place = jnp.where(used, sixteen[None, :], 0)
    local_grid = _lookup(local_atom, grid_position) % ROWS

    def table(right):
        found = jnp.sum(jnp.where(chosen, _lookup(ordered, right)[:, None, :], 0), axis=2)
        right_place = jnp.where(used, found, ATOMS)
        tail = jnp.stack([total, local_grid], axis=1)
        return jnp.concatenate(
            [ranks, right_place, left_place, jnp.pad(tail, ((0, 0), (0, 14)))], axis=1
        )

    return pick_first, pick_rest, table(right_first), table(right_second)


def on_device(atom_blocks, grid_position, pattern):
    scale = 1.0 / math.sqrt(12 * EDGE)
    blocks = atom_blocks[:, 0]
    pick_first, pick_rest, first_table, second_table = build_tables(grid_position, pattern)
    a = move(blocks, MOVE_XA)
    b = move(blocks, MOVE_XB)
    w = move(blocks, MOVE_YP)
    aa = move(a, MOVE_XA)
    wa = move(w, MOVE_XA)
    wb = move(w, MOVE_XB)
    rows_a = pick_rows([blocks, a, b, w], pick_first)
    fa = move(rows_a, MOVE_ZA)
    fb = move(rows_a, MOVE_ZB)
    fy = move(rows_a, MOVE_YA)
    fc = move(rows_a, MOVE_C)
    fh = move(fy, MOVE_YA)
    faa = move(after(fa, fy), MOVE_ZA)
    waa = move(aa, MOVE_YP)
    fca = move(after(fa, fb), MOVE_C)
    fcb = move(fb, MOVE_C)
    fha = move(after(fh, aa), MOVE_ZA)
    fhb = move(after(fh, aa), MOVE_ZB)
    fcaa = move(faa, MOVE_C)
    fch = move(fh, MOVE_C)
    rows_b = pick_rows([wa, wb, aa, waa], pick_rest)
    sa = move(rows_b, MOVE_ZA)
    sb = move(rows_b, MOVE_ZB)
    sy = move(rows_b, MOVE_YA)
    sc = move(rows_b, MOVE_C)
    fhaa = move(after(fha, rows_b), MOVE_ZA)
    fcha = move(after(fha, rows_b), MOVE_C)
    fchb = move(fhb, MOVE_C)
    fchaa = move(fhaa, MOVE_C)
    left_a = [rows_a, fa, fb, fh, fha, fhb, faa, fhaa]
    left_a += [fc, fca, fcb, fch, fcha, fchb, fcaa, fchaa]
    right = [blocks, a, b, w, wa, wb, aa, waa]
    square_a = square_rows(after(first_table[:HALF], sc), left_a, right, scale)
    ga = move(square_a, MOVE_XA)
    gb = move(square_a, MOVE_XB)
    gw = move(square_a, MOVE_YP)
    sh = move(after(sy, square_a), MOVE_YA)
    saa = move(after(sa, square_a), MOVE_ZA)
    sca = move(after(sa, square_a), MOVE_C)
    scb = move(after(sb, square_a), MOVE_C)
    gaa = move(after(ga, sy, sa), MOVE_XA)
    gwa = move(after(gw, sy, sa, gb), MOVE_XA)
    gwb = move(after(gw, sy, sa, gb), MOVE_XB)
    sha = move(after(sh, gw, gb), MOVE_ZA)
    shb = move(after(sh, gw, gb), MOVE_ZB)
    sch = move(sh, MOVE_C)
    scaa = move(saa, MOVE_C)
    gwaa = move(after(gaa, sh), MOVE_YP)
    shaa = move(after(sha, gaa), MOVE_ZA)
    scha = move(after(sha, gaa), MOVE_C)
    schb = move(shb, MOVE_C)
    schaa = move(shaa, MOVE_C)
    left_b = [rows_b, sa, sb, sh, sha, shb, saa, shaa]
    left_b += [sc, sca, scb, sch, scha, schb, scaa, schaa]
    square_b = square_rows(first_table[HALF:], left_b, right, scale)
    ha = move(square_b, MOVE_XA)
    hb = move(square_b, MOVE_XB)
    hw = move(square_b, MOVE_YP)
    haa = move(after(ha, gwa, gwb), MOVE_XA)
    hwa = move(hw, MOVE_XA)
    hwb = move(hw, MOVE_XB)
    hwaa = move(haa, MOVE_YP)
    panel = [square_a, ga, gb, gw, gwa, gwb, gaa, gwaa]
    panel += [square_b, ha, hb, hw, hwa, hwb, haa, hwaa]
    square, update = update_rows(second_table, left_a, left_b, panel, scale)
    return square[:, None], update[:, None]


def solution(mesh):
    in_specs = (P("row", "col", None, None), P(), P())
    out_specs = (P("row", "col", None, None), P("row", "col", None, None))
    return jax.shard_map(
        on_device, mesh=mesh, in_specs=in_specs, out_specs=out_specs, check_vma=False
    )
```

```python
import math

import jax
import jax.numpy as jnp
from jax import lax
from jax.experimental import pallas as pl
from jax.experimental.pallas import tpu as pltpu
from jax.sharding import PartitionSpec as P

AXES = ("row", "col")
NX, NYL, NZ_, NYH, NCORE = 4, 2, 4, 2, 2
ROWS = 16
SLOTS = 16
ATOMS = 128
EDGE = 128
HALF = 8


def _places():
    for x in range(NX):
        for yl in range(NYL):
            for z in range(NZ_):
                for yh in range(NYH):
                    for core in range(NCORE):
                        yield x, yl, z, yh, core


def _linear(x, yl, z, yh, core):
    return (x * NYL + yl) * (NZ_ * NYH * NCORE) + (z * NYH + yh) * NCORE + core


def _moves(step):
    return [(_linear(*p), _linear(*step(*p))) for p in _places()]


def _way(core):
    return 1 if core == 0 else -1


def _y_step(x, yl, z, yh, core):
    y = (yh * NYL + yl + _way(core)) % (NYL * NYH)
    return x, y % NYL, z, y // NYL, core


MOVE_XA = _moves(lambda x, yl, z, yh, c: ((x + _way(c)) % NX, yl, z, yh, c))
MOVE_XB = _moves(lambda x, yl, z, yh, c: ((x - _way(c)) % NX, yl, z, yh, c))
MOVE_YP = _moves(lambda x, yl, z, yh, c: (x, 1 - yl, z, yh, c))
MOVE_ZA = _moves(lambda x, yl, z, yh, c: (x, yl, (z + _way(c)) % NZ_, yh, c))
MOVE_ZB = _moves(lambda x, yl, z, yh, c: (x, yl, (z - _way(c)) % NZ_, yh, c))
MOVE_YA = _moves(_y_step)
MOVE_C = _moves(lambda x, yl, z, yh, c: (x, yl, z, yh, 1 - c))


def move(value, moves, name):
    with jax.named_scope(name):
        return lax.ppermute(value, AXES, moves)


def after(value, *others):
    return lax.optimization_barrier((value, *others))[0]


def _split(value):
    high = value.astype(jnp.bfloat16)
    low = (value - high.astype(jnp.float32)).astype(jnp.bfloat16)
    return high, low


def _pick_kernel(table, *refs):
    n = len(refs) - 2
    pieces, out, sems = refs[:n], refs[n], refs[n + 1]
    copies = []
    for q in range(n):
        for s in range(2):
            e = q * 2 + s
            copies.append(
                pltpu.make_async_copy(
                    pieces[q].at[table[e]], out.at[table[2 * n + e]], sems.at[e]
                )
            )
    for c in copies:
        c.start()
    for c in copies:
        c.wait()


def pick_rows(pieces, table):
    n = len(pieces)
    return pl.pallas_call(
        _pick_kernel,
        out_shape=jax.ShapeDtypeStruct((2 * n, EDGE, EDGE), jnp.float32),
        in_specs=[pl.BlockSpec(memory_space=pltpu.SMEM)]
        + [pl.BlockSpec(memory_space=pltpu.HBM)] * n,
        out_specs=pl.BlockSpec(memory_space=pltpu.VMEM),
        scratch_shapes=[pltpu.SemaphoreType.DMA((2 * n,))],
        compiler_params=pltpu.CompilerParams(vmem_limit_bytes=SMALL_VMEM),
        name="pick_rows",
    )(table, *in_hbm(pieces))


def _start_left(table, left, lbuf, lsem, base, rows):
    def row(local, carry):
        t = base + local
        for p in range(SLOTS):
            rank = table[t, p]

            @pl.when(rank >= 0)
            def _():
                pltpu.make_async_copy(
                    left[p].at[local], lbuf.at[t, rank], lsem.at[t, p]
                ).start()

        return carry

    lax.fori_loop(0, rows, row, 0)


def _product(table, lbuf, rpan, t, start, count):
    ls, rs = [], []
    for n in range(start, start + count):
        ls.append(lbuf[t, table[t, 2 * SLOTS + n]])
        rs.append(rpan[table[t, SLOTS + n]])
    lh, ll = _split(jnp.concatenate(ls, axis=1))
    rh, rl = _split(jnp.concatenate(rs, axis=0))
    four = jnp.dot(
        jnp.concatenate([lh, ll], axis=0),
        jnp.concatenate([rh, rl], axis=1),
        preferred_element_type=jnp.float32,
    )
    return (four[:EDGE, :EDGE] + (four[:EDGE, EDGE:] + four[EDGE:, :EDGE])) + four[
        EDGE:, EDGE:
    ]


def _row_product(table, lbuf, rpan, acc, t):
    total = table[t, 3 * SLOTS]

    @pl.when(total > 0)
    def _():
        acc[...] = _product(table, lbuf, rpan, t, 0, 8)

    @pl.when(total == 0)
    def _():
        acc[...] = jnp.zeros((EDGE, EDGE), jnp.float32)

    @pl.when(total > 8)
    def _():
        acc[...] += _product(table, lbuf, rpan, t, 8, 4)


def _wait_row(table, left, lbuf, lsem, t, local):
    for p in range(SLOTS):
        rank = table[t, p]

        @pl.when(rank >= 0)
        def _():
            pltpu.make_async_copy(
                left[p].at[local], lbuf.at[t, rank], lsem.at[t, p]
            ).wait()


def _stage_kernel(*refs):
    pieces, panel, sems = refs[:-2], refs[-2], refs[-1]
    per = pieces[0].shape[0]
    loads = [
        pltpu.make_async_copy(piece, panel.at[pl.ds(q * per, per)], sems.at[q])
        for q, piece in enumerate(pieces)
    ]
    for c in loads:
        c.start()
    panel[ATOMS] = jnp.zeros((EDGE, EDGE), jnp.float32)
    for c in loads:
        c.wait()


def stage_rows(pieces):
    return pl.pallas_call(
        _stage_kernel,
        out_shape=pltpu.VMEM((ATOMS + 1, EDGE, EDGE), jnp.float32),
        in_specs=[pl.BlockSpec(memory_space=pltpu.HBM)] * len(pieces),
        out_specs=pl.BlockSpec(memory_space=pltpu.VMEM),
        scratch_shapes=[pltpu.SemaphoreType.DMA((len(pieces),))],
        compiler_params=pltpu.CompilerParams(vmem_limit_bytes=SMALL_VMEM),
        name="stage_rows",
    )(*in_hbm(pieces))


def _square_kernel(scale, n_rows, table, *refs):
    left = refs[:SLOTS]
    rpan, out, lbuf, acc, lsem = refs[SLOTS:]
    _start_left(table, left, lbuf, lsem, 0, n_rows)

    def row(t, carry):
        _wait_row(table, left, lbuf, lsem, t, t)
        _row_product(table, lbuf, rpan, acc, t)
        out[t] = acc[...] * scale
        return carry

    lax.fori_loop(0, n_rows, row, 0)


MOST = 12
VMEM_LIMIT = 58 * 2**20
SQUARE_VMEM = 44 * 2**20
SMALL_VMEM = 4 * 2**20


def in_hbm(values):
    return [pltpu.with_memory_space_constraint(v, pltpu.HBM) for v in values]


def square_rows(table, left, panel, scale):
    n_rows = left[0].shape[0]
    return pl.pallas_call(
        lambda *refs: _square_kernel(scale, n_rows, *refs),
        out_shape=jax.ShapeDtypeStruct((n_rows, EDGE, EDGE), jnp.float32),
        in_specs=[pl.BlockSpec(memory_space=pltpu.SMEM)]
        + [pl.BlockSpec(memory_space=pltpu.HBM)] * SLOTS
        + [pl.BlockSpec(memory_space=pltpu.VMEM)],
        out_specs=pl.BlockSpec(memory_space=pltpu.VMEM),
        scratch_shapes=[
            pltpu.VMEM((n_rows, MOST, EDGE, EDGE), jnp.float32),
            pltpu.VMEM((EDGE, EDGE), jnp.float32),
            pltpu.SemaphoreType.DMA((n_rows, SLOTS)),
        ],
        compiler_params=pltpu.CompilerParams(vmem_limit_bytes=SQUARE_VMEM),
        name="square_rows",
    )(table, *in_hbm(left), panel)


def _update_kernel(scale, table, *refs):
    left_a = refs[:SLOTS]
    left_b = refs[SLOTS : 2 * SLOTS]
    right = refs[2 * SLOTS : 2 * SLOTS + 16]
    square, update, lbuf, rpan, acc, ubuf, lsem, rsem, ssem, usem = refs[2 * SLOTS + 16 :]
    loads = [
        pltpu.make_async_copy(right[q], rpan.at[pl.ds(q * HALF, HALF)], rsem.at[q])
        for q in range(16)
    ]
    for c in loads:
        c.start()
    _start_left(table, left_a, lbuf, lsem, 0, HALF)
    _start_left(table, left_b, lbuf, lsem, HALF, HALF)
    rpan[ATOMS] = jnp.zeros((EDGE, EDGE), jnp.float32)
    for c in loads:
        c.wait()
    squares = [
        pltpu.make_async_copy(
            rpan.at[64 * (t // HALF) + t % HALF],
            square.at[table[t, 3 * SLOTS + 1]],
            ssem.at[t],
        )
        for t in range(ROWS)
    ]
    for c in squares:
        c.start()

    def put(t):
        return pltpu.make_async_copy(
            ubuf.at[t], update.at[table[t, 3 * SLOTS + 1]], usem.at[t]
        )

    def rows(left, base):
        def row(local, carry):
            t = base + local
            _wait_row(table, left, lbuf, lsem, t, local)
            _row_product(table, lbuf, rpan, acc, t)
            filled = table[t, 3 * SLOTS] > 0
            ubuf[t] = jnp.where(
                filled, 1.5 * lbuf[t, 0] - (0.5 * scale) * acc[...], 0.0
            )
            put(t).start()
            return carry

        lax.fori_loop(0, HALF, row, 0)

    rows(left_a, 0)
    rows(left_b, HALF)
    for t in range(ROWS):
        put(t).wait()
    for c in squares:
        c.wait()


def update_rows(table, left_a, left_b, right, scale):
    out = jax.ShapeDtypeStruct((ROWS, EDGE, EDGE), jnp.float32)
    hbm = pl.BlockSpec(memory_space=pltpu.HBM)
    return pl.pallas_call(
        lambda *refs: _update_kernel(scale, *refs),
        out_shape=(out, out),
        in_specs=[pl.BlockSpec(memory_space=pltpu.SMEM)] + [hbm] * (2 * SLOTS + 16),
        out_specs=(hbm, hbm),
        scratch_shapes=[
            pltpu.VMEM((ROWS, MOST, EDGE, EDGE), jnp.float32),
            pltpu.VMEM((ATOMS + 1, EDGE, EDGE), jnp.float32),
            pltpu.VMEM((EDGE, EDGE), jnp.float32),
            pltpu.VMEM((ROWS, EDGE, EDGE), jnp.float32),
            pltpu.SemaphoreType.DMA((ROWS, SLOTS)),
            pltpu.SemaphoreType.DMA((16,)),
            pltpu.SemaphoreType.DMA((ROWS,)),
            pltpu.SemaphoreType.DMA((ROWS,)),
        ],
        compiler_params=pltpu.CompilerParams(vmem_limit_bytes=VMEM_LIMIT),
        name="update_rows",
    )(table, *in_hbm(left_a + left_b + right))


def _mod4(v):
    return v & 3


def _order(dx, dy):
    return jnp.where(
        dy == 0,
        jnp.where(dx == 0, 0, jnp.where(dx == 1, 1, jnp.where(dx == 3, 2, 6))),
        jnp.where(dx == 0, 3, jnp.where(dx == 1, 4, jnp.where(dx == 3, 5, 7))),
    )


def _piece(dx, dy, way):
    return _order(_mod4(-way * dx), dy)


def _lookup(keys, values):
    atoms = jnp.arange(ATOMS, dtype=jnp.int32)
    return jnp.sum(jnp.where(keys[..., None] == atoms, values, 0), axis=-1)


def build_tables(grid_position, pattern):
    i32 = jnp.int32
    row = lax.axis_index("row").astype(i32)
    col = lax.axis_index("col").astype(i32)
    x, yl = row // 2, row % 2
    z, yh, core = col // 4, (col // 2) % 2, col % 2
    way = 1 - 2 * core
    atoms = jnp.arange(ATOMS, dtype=i32)
    eights = jnp.arange(8, dtype=i32)
    sixteen = jnp.arange(16, dtype=i32)
    group = atoms // ROWS
    target = grid_position // ROWS
    same = (group[:, None] == group[None, :]) & (target[:, None] == target[None, :])
    rank = jnp.sum((same & (atoms[None, :] < atoms[:, None])).astype(i32), axis=1)
    place = 2 * _order(
        _mod4(group // 2 - target // 2), (group % 2) ^ (target % 2)
    ) + rank
    mine = target == row
    local_atom = jnp.sum(
        jnp.where(mine[None, :] & (place[None, :] == sixteen[:, None]), atoms[None, :], 0),
        axis=1,
    )
    source = _piece(_mod4(group // 2 - x), (group % 2) ^ yl, way)
    pick = 2 * source + rank
    hit = mine[None, :] & (pick[None, :] == sixteen[:, None])
    pick_row = jnp.sum(jnp.where(hit, (atoms % ROWS)[None, :], 0), axis=1)
    pick_place = jnp.sum(jnp.where(hit, place[None, :], 0), axis=1)
    pick_first = jnp.concatenate([pick_row[:HALF], pick_place[:HALF]])
    pick_rest = jnp.concatenate([pick_row[HALF:], pick_place[HALF:] - HALF])
    right_first = source * ROWS + atoms % ROWS
    holder = _piece(_mod4(target // 2 - x), (target % 2) ^ yl, way)
    right_second = (place // HALF) * 64 + holder * HALF + place % HALF
    def slots(d, c):
        dz = jnp.stack([0 * d, -d, d, 0 * d, -d, d, 0 * d + 2, 0 * d + 2])
        flip = jnp.where(((eights >= 3) & (eights <= 5)) | (eights == 7), 1, 0)
        return _mod4(z + dz) * 4 + (yh ^ flip) * 2 + c

    slot_of = jnp.concatenate([slots(way, core), slots(-way, 1 - core)])
    column = lax.dynamic_slice_in_dim(pattern, col, 1, 1)[:, 0]
    local_pattern = jnp.sum(
        jnp.where((local_atom[:, None] == atoms)[:, :, None], pattern[None], 0), axis=1
    )
    ordered = jnp.sum(
        jnp.where((slot_of[:, None] == sixteen)[None], local_pattern[:, None, :], 0),
        axis=2,
    )
    mine_column = ordered[:, :1]
    match = (ordered >= 0) & (mine_column >= 0) & (_lookup(ordered, column) == mine_column)
    counts = match.astype(i32)
    before = jnp.sum(
        jnp.where(sixteen[None, None, :] < sixteen[None, :, None], counts[:, None, :], 0),
        axis=2,
    )
    total = jnp.sum(counts, axis=1)
    ranks = jnp.where(match, before, -1)
    chosen = ranks[:, None, :] == sixteen[None, :, None]
    used = sixteen[None, :] < total[:, None]
    left_place = jnp.where(used, sixteen[None, :], 0)
    local_grid = _lookup(local_atom, grid_position) % ROWS

    def table(right):
        found = jnp.sum(jnp.where(chosen, _lookup(ordered, right)[:, None, :], 0), axis=2)
        right_place = jnp.where(used, found, ATOMS)
        tail = jnp.stack([total, local_grid], axis=1)
        return jnp.concatenate(
            [ranks, right_place, left_place, jnp.pad(tail, ((0, 0), (0, 14)))], axis=1
        )

    return pick_first, pick_rest, table(right_first), table(right_second)


def on_device(atom_blocks, grid_position, pattern):
    scale = 1.0 / math.sqrt(12 * EDGE)
    blocks = atom_blocks[:, 0]
    pick_first, pick_rest, first_table, second_table = build_tables(grid_position, pattern)
    a = move(blocks, MOVE_XA, "a")
    b = move(blocks, MOVE_XB, "b")
    w = move(blocks, MOVE_YP, "w")
    aa = move(a, MOVE_XA, "aa")
    wa = move(w, MOVE_XA, "wa")
    wb = move(w, MOVE_XB, "wb")
    rows_a = pick_rows([blocks, a, b, w], pick_first)
    fa = move(rows_a, MOVE_ZA, "fa")
    fb = move(rows_a, MOVE_ZB, "fb")
    fy = move(rows_a, MOVE_YA, "fy")
    fc = move(rows_a, MOVE_C, "fc")
    fh = move(fy, MOVE_YA, "fh")
    faa = move(after(fa, fy), MOVE_ZA, "faa")
    waa = move(aa, MOVE_YP, "waa")
    fca = move(after(fa, fb), MOVE_C, "fca")
    fcb = move(fb, MOVE_C, "fcb")
    fha = move(after(fh, aa), MOVE_ZA, "fha")
    fhb = move(after(fh, aa), MOVE_ZB, "fhb")
    fcaa = move(faa, MOVE_C, "fcaa")
    fch = move(fh, MOVE_C, "fch")
    rows_b = pick_rows([wa, wb, aa, waa], pick_rest)
    sa = move(rows_b, MOVE_ZA, "sa")
    sb = move(rows_b, MOVE_ZB, "sb")
    sy = move(rows_b, MOVE_YA, "sy")
    sc = move(rows_b, MOVE_C, "sc")
    staged = stage_rows([blocks, a, b, w, wa, wb, aa, waa])
    fhaa = move(after(fha, rows_b), MOVE_ZA, "fhaa")
    fcha = move(after(fha, rows_b), MOVE_C, "fcha")
    fchb = move(fhb, MOVE_C, "fchb")
    fchaa = move(fhaa, MOVE_C, "fchaa")
    left_a = [rows_a, fa, fb, fh, fha, fhb, faa, fhaa]
    left_a += [fc, fca, fcb, fch, fcha, fchb, fcaa, fchaa]
    square_a = square_rows(after(first_table[:HALF], sc), left_a, staged, scale)
    ga = move(square_a, MOVE_XA, "ga")
    gb = move(square_a, MOVE_XB, "gb")
    gw = move(square_a, MOVE_YP, "gw")
    sh = move(after(sy, square_a), MOVE_YA, "sh")
    saa = move(after(sa, square_a), MOVE_ZA, "saa")
    sca = move(after(sa, square_a), MOVE_C, "sca")
    scb = move(after(sb, square_a), MOVE_C, "scb")
    gaa = move(after(ga, sy, sa), MOVE_XA, "gaa")
    gwa = move(after(gw, sy, sa, gb), MOVE_XA, "gwa")
    gwb = move(after(gw, sy, sa, gb), MOVE_XB, "gwb")
    sha = move(after(sh, gw, gb), MOVE_ZA, "sha")
    shb = move(after(sh, gw, gb), MOVE_ZB, "shb")
    sch = move(sh, MOVE_C, "sch")
    scaa = move(saa, MOVE_C, "scaa")
    gwaa = move(after(gaa, sh), MOVE_YP, "gwaa")
    shaa = move(after(sha, gaa), MOVE_ZA, "shaa")
    scha = move(after(sha, gaa), MOVE_C, "scha")
    schb = move(shb, MOVE_C, "schb")
    schaa = move(shaa, MOVE_C, "schaa")
    left_b = [rows_b, sa, sb, sh, sha, shb, saa, shaa]
    left_b += [sc, sca, scb, sch, scha, schb, scaa, schaa]
    square_b = square_rows(first_table[HALF:], left_b, staged, scale)
    ha = move(square_b, MOVE_XA, "ha")
    hb = move(square_b, MOVE_XB, "hb")
    hw = move(square_b, MOVE_YP, "hw")
    haa = move(after(ha, gwa, gwb), MOVE_XA, "haa")
    hwa = move(hw, MOVE_XA, "hwa")
    hwb = move(hw, MOVE_XB, "hwb")
    hwaa = move(haa, MOVE_YP, "hwaa")
    panel = [square_a, ga, gb, gw, gwa, gwb, gaa, gwaa]
    panel += [square_b, ha, hb, hw, hwa, hwb, haa, hwaa]
    square, update = update_rows(second_table, left_a, left_b, panel, scale)
    return square[:, None], update[:, None]


def solution(mesh):
    in_specs = (P("row", "col", None, None), P(), P())
    out_specs = (P("row", "col", None, None), P("row", "col", None, None))
    return jax.shard_map(
        on_device, mesh=mesh, in_specs=in_specs, out_specs=out_specs, check_vma=False
    )
```

```python
import math

import jax
import jax.numpy as jnp
from jax import lax
from jax.experimental import pallas as pl
from jax.experimental.pallas import tpu as pltpu
from jax.sharding import PartitionSpec as P

AXES = ("row", "col")
NX, NYL, NZ_, NYH, NCORE = 4, 2, 4, 2, 2
ROWS = 16
SLOTS = 16
ATOMS = 128
EDGE = 128
HALF = 8


def _places():
    for x in range(NX):
        for yl in range(NYL):
            for z in range(NZ_):
                for yh in range(NYH):
                    for core in range(NCORE):
                        yield x, yl, z, yh, core


def _linear(x, yl, z, yh, core):
    return (x * NYL + yl) * (NZ_ * NYH * NCORE) + (z * NYH + yh) * NCORE + core


def _moves(step):
    return [(_linear(*p), _linear(*step(*p))) for p in _places()]


def _way(core):
    return 1 if core == 0 else -1


def _y_step(x, yl, z, yh, core):
    y = (yh * NYL + yl + _way(core)) % (NYL * NYH)
    return x, y % NYL, z, y // NYL, core


MOVE_XA = _moves(lambda x, yl, z, yh, c: ((x + _way(c)) % NX, yl, z, yh, c))
MOVE_XB = _moves(lambda x, yl, z, yh, c: ((x - _way(c)) % NX, yl, z, yh, c))
MOVE_YP = _moves(lambda x, yl, z, yh, c: (x, 1 - yl, z, yh, c))
MOVE_ZA = _moves(lambda x, yl, z, yh, c: (x, yl, (z + _way(c)) % NZ_, yh, c))
MOVE_ZB = _moves(lambda x, yl, z, yh, c: (x, yl, (z - _way(c)) % NZ_, yh, c))
MOVE_YA = _moves(_y_step)
MOVE_C = _moves(lambda x, yl, z, yh, c: (x, yl, z, yh, 1 - c))


def move(value, moves, name):
    with jax.named_scope(name):
        return lax.ppermute(value, AXES, moves)


def after(value, *others):
    return lax.optimization_barrier((value, *others))[0]


def _split(value):
    high = value.astype(jnp.bfloat16)
    low = (value - high.astype(jnp.float32)).astype(jnp.bfloat16)
    return high, low


def _pick_kernel(table, *refs):
    n = len(refs) - 2
    pieces, out, sems = refs[:n], refs[n], refs[n + 1]
    copies = []
    for q in range(n):
        for s in range(2):
            e = q * 2 + s
            copies.append(
                pltpu.make_async_copy(
                    pieces[q].at[table[e]], out.at[table[2 * n + e]], sems.at[e]
                )
            )
    for c in copies:
        c.start()
    for c in copies:
        c.wait()


def pick_rows(pieces, table):
    n = len(pieces)
    return pl.pallas_call(
        _pick_kernel,
        out_shape=jax.ShapeDtypeStruct((2 * n, EDGE, EDGE), jnp.float32),
        in_specs=[pl.BlockSpec(memory_space=pltpu.SMEM)]
        + [pl.BlockSpec(memory_space=pltpu.HBM)] * n,
        out_specs=pl.BlockSpec(memory_space=pltpu.VMEM),
        scratch_shapes=[pltpu.SemaphoreType.DMA((2 * n,))],
        compiler_params=pltpu.CompilerParams(vmem_limit_bytes=SMALL_VMEM),
        name="pick_rows",
    )(table, *pieces)


def _start_left(table, left, lbuf, lsem, base, rows):
    def row(local, carry):
        t = base + local
        for p in range(SLOTS):
            rank = table[t, p]

            @pl.when(rank >= 0)
            def _():
                pltpu.make_async_copy(
                    left[p].at[local], lbuf.at[t, rank], lsem.at[t, p]
                ).start()

        return carry

    lax.fori_loop(0, rows, row, 0)


def _product(table, lbuf, rpan, t, start, count):
    ls, rs = [], []
    for n in range(start, start + count):
        ls.append(lbuf[t, table[t, 2 * SLOTS + n]])
        rs.append(rpan[table[t, SLOTS + n]])
    lh, ll = _split(jnp.concatenate(ls, axis=1))
    rh, rl = _split(jnp.concatenate(rs, axis=0))
    four = jnp.dot(
        jnp.concatenate([lh, ll], axis=0),
        jnp.concatenate([rh, rl], axis=1),
        preferred_element_type=jnp.float32,
    )
    return (four[:EDGE, :EDGE] + (four[:EDGE, EDGE:] + four[EDGE:, :EDGE])) + four[
        EDGE:, EDGE:
    ]


def _row_product(table, lbuf, rpan, acc, t):
    total = table[t, 3 * SLOTS]

    @pl.when(total > 0)
    def _():
        acc[...] = _product(table, lbuf, rpan, t, 0, 8)

    @pl.when(total == 0)
    def _():
        acc[...] = jnp.zeros((EDGE, EDGE), jnp.float32)

    @pl.when(total > 8)
    def _():
        acc[...] += _product(table, lbuf, rpan, t, 8, 4)


def _wait_row(table, left, lbuf, lsem, t, local):
    for p in range(SLOTS):
        rank = table[t, p]

        @pl.when(rank >= 0)
        def _():
            pltpu.make_async_copy(
                left[p].at[local], lbuf.at[t, rank], lsem.at[t, p]
            ).wait()


def _stage_kernel(*refs):
    pieces, panel, sems = refs[:-2], refs[-2], refs[-1]
    per = pieces[0].shape[0]
    loads = [
        pltpu.make_async_copy(piece, panel.at[pl.ds(q * per, per)], sems.at[q])
        for q, piece in enumerate(pieces)
    ]
    for c in loads:
        c.start()
    panel[ATOMS] = jnp.zeros((EDGE, EDGE), jnp.float32)
    for c in loads:
        c.wait()


def stage_rows(pieces):
    return pl.pallas_call(
        _stage_kernel,
        out_shape=pltpu.VMEM((ATOMS + 1, EDGE, EDGE), jnp.float32),
        in_specs=[pl.BlockSpec(memory_space=pltpu.HBM)] * len(pieces),
        out_specs=pl.BlockSpec(memory_space=pltpu.VMEM),
        scratch_shapes=[pltpu.SemaphoreType.DMA((len(pieces),))],
        compiler_params=pltpu.CompilerParams(vmem_limit_bytes=SMALL_VMEM),
        name="stage_rows",
    )(*in_hbm(pieces))


def _square_kernel(scale, n_rows, table, *refs):
    left = refs[:SLOTS]
    rpan, out, lbuf, acc, lsem = refs[SLOTS:]
    _start_left(table, left, lbuf, lsem, 0, n_rows)

    def row(t, carry):
        _wait_row(table, left, lbuf, lsem, t, t)
        _row_product(table, lbuf, rpan, acc, t)
        out[t] = acc[...] * scale
        return carry

    lax.fori_loop(0, n_rows, row, 0)


MOST = 12
VMEM_LIMIT = 58 * 2**20
SQUARE_VMEM = 44 * 2**20
SMALL_VMEM = 4 * 2**20


def in_hbm(values):
    return [pltpu.with_memory_space_constraint(v, pltpu.HBM) for v in values]


def square_rows(table, left, panel, scale):
    n_rows = left[0].shape[0]
    return pl.pallas_call(
        lambda *refs: _square_kernel(scale, n_rows, *refs),
        out_shape=jax.ShapeDtypeStruct((n_rows, EDGE, EDGE), jnp.float32),
        in_specs=[pl.BlockSpec(memory_space=pltpu.SMEM)]
        + [pl.BlockSpec(memory_space=pltpu.HBM)] * SLOTS
        + [pl.BlockSpec(memory_space=pltpu.VMEM)],
        out_specs=pl.BlockSpec(memory_space=pltpu.VMEM),
        scratch_shapes=[
            pltpu.VMEM((n_rows, MOST, EDGE, EDGE), jnp.float32),
            pltpu.VMEM((EDGE, EDGE), jnp.float32),
            pltpu.SemaphoreType.DMA((n_rows, SLOTS)),
        ],
        compiler_params=pltpu.CompilerParams(vmem_limit_bytes=SQUARE_VMEM),
        name="square_rows",
    )(table, *in_hbm(left), panel)


def _update_kernel(scale, table, *refs):
    left_a = refs[:SLOTS]
    left_b = refs[SLOTS : 2 * SLOTS]
    right = refs[2 * SLOTS + 1 : 2 * SLOTS + 9]
    square, update, rpan, lbuf, acc, ubuf, lsem, rsem, ssem, usem = refs[2 * SLOTS + 9 :]
    loads = [
        pltpu.make_async_copy(right[q], rpan.at[pl.ds(64 + q * HALF, HALF)], rsem.at[q])
        for q in range(8)
    ]
    for c in loads:
        c.start()
    _start_left(table, left_a, lbuf, lsem, 0, HALF)
    _start_left(table, left_b, lbuf, lsem, HALF, HALF)
    for c in loads:
        c.wait()
    squares = [
        pltpu.make_async_copy(
            rpan.at[64 * (t // HALF) + t % HALF],
            square.at[table[t, 3 * SLOTS + 1]],
            ssem.at[t],
        )
        for t in range(ROWS)
    ]
    for c in squares:
        c.start()

    def put(t):
        return pltpu.make_async_copy(
            ubuf.at[t], update.at[table[t, 3 * SLOTS + 1]], usem.at[t]
        )

    def rows(left, base):
        def row(local, carry):
            t = base + local
            _wait_row(table, left, lbuf, lsem, t, local)
            _row_product(table, lbuf, rpan, acc, t)
            filled = table[t, 3 * SLOTS] > 0
            ubuf[t] = jnp.where(
                filled, 1.5 * lbuf[t, 0] - (0.5 * scale) * acc[...], 0.0
            )
            put(t).start()
            return carry

        lax.fori_loop(0, HALF, row, 0)

    rows(left_a, 0)
    rows(left_b, HALF)
    for t in range(ROWS):
        put(t).wait()
    for c in squares:
        c.wait()


def update_rows(table, left_a, left_b, staged, right, scale):
    out = jax.ShapeDtypeStruct((ROWS, EDGE, EDGE), jnp.float32)
    hbm = pl.BlockSpec(memory_space=pltpu.HBM)
    vmem = pl.BlockSpec(memory_space=pltpu.VMEM)
    return pl.pallas_call(
        lambda *refs: _update_kernel(scale, *refs),
        out_shape=(out, out, pltpu.VMEM((ATOMS + 1, EDGE, EDGE), jnp.float32)),
        input_output_aliases={1 + 2 * SLOTS: 2},
        in_specs=[pl.BlockSpec(memory_space=pltpu.SMEM)] + [hbm] * (2 * SLOTS) + [vmem] + [hbm] * 8,
        out_specs=(hbm, hbm, vmem),
        scratch_shapes=[
            pltpu.VMEM((ROWS, MOST, EDGE, EDGE), jnp.float32),
            pltpu.VMEM((EDGE, EDGE), jnp.float32),
            pltpu.VMEM((ROWS, EDGE, EDGE), jnp.float32),
            pltpu.SemaphoreType.DMA((ROWS, SLOTS)),
            pltpu.SemaphoreType.DMA((16,)),
            pltpu.SemaphoreType.DMA((ROWS,)),
            pltpu.SemaphoreType.DMA((ROWS,)),
        ],
        compiler_params=pltpu.CompilerParams(vmem_limit_bytes=SQUARE_VMEM),
        name="update_rows",
    )(table, *in_hbm(left_a + left_b), staged, *in_hbm(right))


def _mod4(v):
    return v & 3


def _order(dx, dy):
    return jnp.where(
        dy == 0,
        jnp.where(dx == 0, 0, jnp.where(dx == 1, 1, jnp.where(dx == 3, 2, 6))),
        jnp.where(dx == 0, 3, jnp.where(dx == 1, 4, jnp.where(dx == 3, 5, 7))),
    )


def _piece(dx, dy, way):
    return _order(_mod4(-way * dx), dy)


def _lookup(keys, values):
    atoms = jnp.arange(ATOMS, dtype=jnp.int32)
    return jnp.sum(jnp.where(keys[..., None] == atoms, values, 0), axis=-1)


def build_tables(grid_position, pattern):
    i32 = jnp.int32
    row = lax.axis_index("row").astype(i32)
    col = lax.axis_index("col").astype(i32)
    x, yl = row // 2, row % 2
    z, yh, core = col // 4, (col // 2) % 2, col % 2
    way = 1 - 2 * core
    atoms = jnp.arange(ATOMS, dtype=i32)
    eights = jnp.arange(8, dtype=i32)
    sixteen = jnp.arange(16, dtype=i32)
    group = atoms // ROWS
    target = grid_position // ROWS
    same = (group[:, None] == group[None, :]) & (target[:, None] == target[None, :])
    rank = jnp.sum((same & (atoms[None, :] < atoms[:, None])).astype(i32), axis=1)
    place = 2 * _order(
        _mod4(group // 2 - target // 2), (group % 2) ^ (target % 2)
    ) + rank
    mine = target == row
    local_atom = jnp.sum(
        jnp.where(mine[None, :] & (place[None, :] == sixteen[:, None]), atoms[None, :], 0),
        axis=1,
    )
    source = _piece(_mod4(group // 2 - x), (group % 2) ^ yl, way)
    pick = 2 * source + rank
    hit = mine[None, :] & (pick[None, :] == sixteen[:, None])
    pick_row = jnp.sum(jnp.where(hit, (atoms % ROWS)[None, :], 0), axis=1)
    pick_place = jnp.sum(jnp.where(hit, place[None, :], 0), axis=1)
    pick_first = jnp.concatenate([pick_row[:HALF], pick_place[:HALF]])
    pick_rest = jnp.concatenate([pick_row[HALF:], pick_place[HALF:] - HALF])
    right_first = source * ROWS + atoms % ROWS
    holder = _piece(_mod4(target // 2 - x), (target % 2) ^ yl, way)
    right_second = (place // HALF) * 64 + holder * HALF + place % HALF
    def slots(d, c):
        dz = jnp.stack([0 * d, -d, d, 0 * d, -d, d, 0 * d + 2, 0 * d + 2])
        flip = jnp.where(((eights >= 3) & (eights <= 5)) | (eights == 7), 1, 0)
        return _mod4(z + dz) * 4 + (yh ^ flip) * 2 + c

    slot_of = jnp.concatenate([slots(way, core), slots(-way, 1 - core)])
    column = lax.dynamic_slice_in_dim(pattern, col, 1, 1)[:, 0]
    local_pattern = jnp.sum(
        jnp.where((local_atom[:, None] == atoms)[:, :, None], pattern[None], 0), axis=1
    )
    ordered = jnp.sum(
        jnp.where((slot_of[:, None] == sixteen)[None], local_pattern[:, None, :], 0),
        axis=2,
    )
    mine_column = ordered[:, :1]
    match = (ordered >= 0) & (mine_column >= 0) & (_lookup(ordered, column) == mine_column)
    counts = match.astype(i32)
    before = jnp.sum(
        jnp.where(sixteen[None, None, :] < sixteen[None, :, None], counts[:, None, :], 0),
        axis=2,
    )
    total = jnp.sum(counts, axis=1)
    ranks = jnp.where(match, before, -1)
    chosen = ranks[:, None, :] == sixteen[None, :, None]
    used = sixteen[None, :] < total[:, None]
    left_place = jnp.where(used, sixteen[None, :], 0)
    local_grid = _lookup(local_atom, grid_position) % ROWS

    def table(right):
        found = jnp.sum(jnp.where(chosen, _lookup(ordered, right)[:, None, :], 0), axis=2)
        right_place = jnp.where(used, found, ATOMS)
        tail = jnp.stack([total, local_grid], axis=1)
        return jnp.concatenate(
            [ranks, right_place, left_place, jnp.pad(tail, ((0, 0), (0, 14)))], axis=1
        )

    return pick_first, pick_rest, table(right_first), table(right_second)


def on_device(atom_blocks, grid_position, pattern):
    scale = 1.0 / math.sqrt(12 * EDGE)
    blocks = atom_blocks[:, 0]
    pick_first, pick_rest, first_table, second_table = build_tables(grid_position, pattern)
    a = move(blocks, MOVE_XA, "a")
    b = move(blocks, MOVE_XB, "b")
    w = move(blocks, MOVE_YP, "w")
    aa = move(a, MOVE_XA, "aa")
    wa = move(w, MOVE_XA, "wa")
    wb = move(w, MOVE_XB, "wb")
    rows_a = pick_rows([blocks, a, b, w], pick_first)
    fa = move(rows_a, MOVE_ZA, "fa")
    fb = move(rows_a, MOVE_ZB, "fb")
    fy = move(rows_a, MOVE_YA, "fy")
    fc = move(rows_a, MOVE_C, "fc")
    fh = move(fy, MOVE_YA, "fh")
    faa = move(after(fa, fy), MOVE_ZA, "faa")
    waa = move(aa, MOVE_YP, "waa")
    fca = move(after(fa, fb), MOVE_C, "fca")
    fcb = move(fb, MOVE_C, "fcb")
    fha = move(after(fh, aa), MOVE_ZA, "fha")
    fhb = move(after(fh, aa), MOVE_ZB, "fhb")
    fcaa = move(faa, MOVE_C, "fcaa")
    fch = move(fh, MOVE_C, "fch")
    rows_b = pick_rows([wa, wb, aa, waa], pick_rest)
    sa = move(rows_b, MOVE_ZA, "sa")
    sb = move(rows_b, MOVE_ZB, "sb")
    sy = move(rows_b, MOVE_YA, "sy")
    sc = move(rows_b, MOVE_C, "sc")
    staged = stage_rows([blocks, a, b, w, wa, wb, aa, waa])
    fhaa = move(after(fha, rows_b), MOVE_ZA, "fhaa")
    fcha = move(after(fha, rows_b), MOVE_C, "fcha")
    fchb = move(fhb, MOVE_C, "fchb")
    fchaa = move(fhaa, MOVE_C, "fchaa")
    left_a = [rows_a, fa, fb, fh, fha, fhb, faa, fhaa]
    left_a += [fc, fca, fcb, fch, fcha, fchb, fcaa, fchaa]
    square_a = square_rows(after(first_table[:HALF], sc), left_a, staged, scale)
    ga = move(square_a, MOVE_XA, "ga")
    gb = move(square_a, MOVE_XB, "gb")
    gw = move(square_a, MOVE_YP, "gw")
    sh = move(after(sy, square_a), MOVE_YA, "sh")
    saa = move(after(sa, square_a), MOVE_ZA, "saa")
    sca = move(after(sa, square_a), MOVE_C, "sca")
    scb = move(after(sb, square_a), MOVE_C, "scb")
    gaa = move(after(ga, sy, sa), MOVE_XA, "gaa")
    gwa = move(after(gw, sy, sa, gb), MOVE_XA, "gwa")
    gwb = move(after(gw, sy, sa, gb), MOVE_XB, "gwb")
    sha = move(after(sh, gw, gb), MOVE_ZA, "sha")
    shb = move(after(sh, gw, gb), MOVE_ZB, "shb")
    sch = move(sh, MOVE_C, "sch")
    scaa = move(saa, MOVE_C, "scaa")
    gwaa = move(after(gaa, sh), MOVE_YP, "gwaa")
    shaa = move(after(sha, gaa), MOVE_ZA, "shaa")
    scha = move(after(sha, gaa), MOVE_C, "scha")
    schb = move(shb, MOVE_C, "schb")
    schaa = move(shaa, MOVE_C, "schaa")
    left_b = [rows_b, sa, sb, sh, sha, shb, saa, shaa]
    left_b += [sc, sca, scb, sch, scha, schb, scaa, schaa]
    square_b = square_rows(first_table[HALF:], left_b, staged, scale)
    ha = move(square_b, MOVE_XA, "ha")
    hb = move(square_b, MOVE_XB, "hb")
    hw = move(square_b, MOVE_YP, "hw")
    haa = move(after(ha, gwa, gwb), MOVE_XA, "haa")
    hwa = move(hw, MOVE_XA, "hwa")
    hwb = move(hw, MOVE_XB, "hwb")
    staged = stage_rows([square_a, ga, gb, gw, gwa, gwb, gaa, gwaa])
    hwaa = move(haa, MOVE_YP, "hwaa")
    panel_b = [square_b, ha, hb, hw, hwa, hwb, haa, hwaa]
    square, update, _ = update_rows(second_table, left_a, left_b, staged, panel_b, scale)
    return square[:, None], update[:, None]


def solution(mesh):
    in_specs = (P("row", "col", None, None), P(), P())
    out_specs = (P("row", "col", None, None), P("row", "col", None, None))
    return jax.shard_map(
        on_device, mesh=mesh, in_specs=in_specs, out_specs=out_specs, check_vma=False
    )
```
